32 devices in a mesh: space: 4 (over y, x), mode: 8 (over z, core).
Axes of the slice: x: 2, y: 2, z: 4, core: 2. Of those that a mesh axis runs over, the one named last changes fastest.
Arguments:
- source_field: float32 [8, 4, 128, 2048], P('space', None, None, 'mode'), may hold values from -6 to 6
- mean_operator: float32 [8, 4, 128, 896], P('space'), may hold values from -0.109375 to 0.109375
- field_operators: float32 [4, 8, 4, 128, 896], P(None, 'space'), may hold values from -0.078125 to 0.078125
- adjacency: int32 [8, 4, 4], P('space'), may hold values from 0 to 3
- mode_masks: int32 [4], replicated, may hold values from 256 to 1024, as said below
Outputs:
- solution_field: float32 [8, 4, 128, 2048], P('space', None, None, 'mode')
- residual: float32 [8, 4, 128, 2048], P('space', None, None, 'mode')
The draws below stay inside these ranges and needn't reach their ends.
Inputs may be any that keep to these rules, and one draw needn't show every extreme that they name: `mode_masks`: each value is 256 times a power of two, at most 1024, and every such value belongs to at least one field.
All inputs are finite; a program needn't handle non-finite values.
Results may differ from the reference program's by a relative error of at most 0.0001.
Values sent between devices are 32-bit elements; how exact they have to be, the bound alone decides.
A program may use at most 128 MiB of HBM per device.

```python
import jax
import jax.numpy as jnp
from jax import lax

BLK = 128
MODE_DEV = 256
MODES = 2048
NF = 4
FACE = 4
LAYERS = 8
DEGREE = 4


def draw_mode_masks(key, part):
    bit_count = (MODES // MODE_DEV).bit_length() - 1
    order = jax.random.permutation(jax.random.fold_in(key, 11), NF)
    extra = jax.random.randint(jax.random.fold_in(key, 12), (NF,), 0, bit_count)
    slots = jnp.arange(NF, dtype=jnp.int32)
    slot_bits = jnp.where(slots < bit_count, slots, extra)
    field_bits = slot_bits[order]
    return (MODE_DEV * jnp.left_shift(jnp.ones((NF,), jnp.int32), field_bits)).astype(jnp.int32)


def with_ends(values, rng, low, largest):
    shape = values.shape
    index_at = [jax.random.randint(jax.random.fold_in(rng, axis), (), 0, shape[axis]) for axis in range(len(shape))]
    values = values.at[tuple(index_at)].set(low)
    longest = shape.index(max(shape))
    index_at[longest] = (index_at[longest] + 1) % shape[longest]
    return values.at[tuple(index_at)].set(largest)


def level_of(key, shape, pieces, low, top_value):
    loudness, own = 1.0, jax.random.fold_in(key, 6)
    for axis_at, shards_of in pieces:
        draws = jnp.exp(jax.random.uniform(jax.random.fold_in(own, axis_at), (shards_of,), jnp.float32, low / len(pieces), top_value / len(pieces)))
        loudness = loudness * jnp.repeat(draws, shape[axis_at] // shards_of).reshape([-1 if axis == axis_at else 1 for axis in range(len(shape))])
    return loudness


def gaussian(own_key, shape, deviation, limit, split=(), kind=jnp.bfloat16):
    factor_of = level_of(own_key, shape, split, -0.22, 0.18) if split else 1.0
    array = jax.random.normal(own_key, shape, jnp.float32) * deviation * factor_of
    return jnp.minimum(jnp.maximum(array, -limit), limit).astype(kind)


def setup_inputs(seed: int = 0) -> dict:
    streams_of = jax.random.split(jax.random.key(seed), 6)
    return {
        "source_field": gaussian(streams_of[0], (LAYERS, FACE, BLK, MODES), 1.0, 6.0, ((0, 4), (3, 8)), jnp.float32),
        "mean_operator": gaussian(streams_of[1], (LAYERS, FACE, BLK, 7 * BLK), 0.007, 0.109375, ((0, 4),), jnp.float32),
        "field_operators": gaussian(streams_of[2], (NF, LAYERS, FACE, BLK, 7 * BLK), 0.005, 0.078125, ((1, 4),), jnp.float32),
        "adjacency": with_ends(jax.random.randint(streams_of[3], (LAYERS, FACE, 4), 0, FACE), jax.random.fold_in(streams_of[3], 1), 0, FACE - 1).astype(jnp.int32),
        "mode_masks": draw_mode_masks(jax.random.fold_in(streams_of[5], 71), 0),
    }


coupling_coef = 0.5773502691896258
theta_value = 1.0
delta_value = 0.7


def operate_on(field, mean_operator, field_operators, adjacency, mode_masks):
    padded = jnp.pad(field, ((1, 1), (0, 0), (0, 0), (0, 0)))
    mode_index = jnp.arange(field.shape[3], dtype=jnp.int32)

    def one_layer(layer_index):
        window = lax.dynamic_slice_in_dim(padded, layer_index, 3, 0)
        centre = window[1]
        neighbours = adjacency[layer_index]
        in_layer = centre[neighbours]
        stacked = jnp.concatenate([centre[:, None], window[0][:, None], window[2][:, None], in_layer], axis=1)
        columns = stacked.reshape(FACE, 7 * BLK, field.shape[3])
        result = centre + jnp.einsum("fij,fjm->fim", mean_operator[layer_index], columns, precision=lax.Precision.HIGHEST)
        for field_number in range(NF):
            term = jnp.einsum("fij,fjm->fim", field_operators[field_number, layer_index], columns, precision=lax.Precision.HIGHEST)
            partner = jnp.bitwise_xor(mode_index, mode_masks[field_number])
            result = result + coupling_coef * jnp.take(term, partner, axis=2)
        return result

    return lax.map(one_layer, jnp.arange(LAYERS, dtype=jnp.int32))


def reference(source_field, mean_operator, field_operators, adjacency, mode_masks):
    sigma_value = theta_value / delta_value
    solution_field = jnp.zeros_like(source_field)
    residual = source_field
    direction = source_field / theta_value
    ratio_now = jnp.asarray(1.0 / sigma_value, dtype=jnp.float32)

    def iterate_once(count, carry):
        solution_field, residual, direction, ratio_now = carry
        solution_field = solution_field + direction
        residual = residual - operate_on(direction, mean_operator, field_operators, adjacency, mode_masks)
        ratio_new = 1.0 / (2.0 * sigma_value - ratio_now)
        direction = ratio_new * ratio_now * direction + (2.0 * ratio_new / delta_value) * residual
        return solution_field, residual, direction, ratio_new

    solution_field, residual, direction, ratio_now = lax.fori_loop(0, DEGREE, iterate_once, (solution_field, residual, direction, ratio_now))
    return solution_field, residual
```

```python
import functools

import jax
import jax.numpy as jnp
from jax import lax
from jax.experimental import pallas as pl
from jax.experimental.pallas import tpu as pltpu
from jax.sharding import PartitionSpec as P

DEGREE = 4
COUPLING = 0.5773502691896258
THETA = 1.0
DELTA = 0.7
CHUNKS = 2
VMEM_LIMIT = 66_000_000
MESH = pl.DeviceIdType.MESH


def prep_kernel(face, bits, modes_dev, mean_ref, field_ref, adj_ref, mask_ref, hi_ref, lo_ref):
    layer, f = pl.program_id(0), pl.program_id(1)
    blk = mean_ref.shape[2]
    fields = field_ref.shape[0]
    for op in range(bits + 1):
        if op == 0:
            whole = mean_ref[0, 0]
        else:
            whole = jnp.zeros(mean_ref.shape[2:], jnp.float32)
            for j in range(fields):
                weight = jnp.where(mask_ref[j] == modes_dev * (1 << (op - 1)), COUPLING, 0.0).astype(jnp.float32)
                whole = whole + weight * field_ref[j, 0, 0]
        block = lambda s: whole[:, s * blk : (s + 1) * blk]
        parts = []
        for g in range(face):
            total = jnp.where(f == g, 1.0, 0.0).astype(jnp.float32) * block(0)
            for s in range(adj_ref.shape[2]):
                here = jnp.where(adj_ref[layer, f, s] == g, 1.0, 0.0).astype(jnp.float32)
                total = total + here * block(3 + s)
            parts.append(total)
        parts += [block(1), block(2)]
        for at, part in enumerate(parts):
            high = part.astype(jnp.bfloat16)
            low = (part - high.astype(jnp.float32)).astype(jnp.bfloat16)
            hi_ref[0, 0, op * blk : (op + 1) * blk, at * blk : (at + 1) * blk] = high
            lo_ref[0, 0, op * blk : (op + 1) * blk, at * blk : (at + 1) * blk] = low


def prepared(mean_operator, field_operators, adjacency, mode_masks, bits, modes_dev):
    layers, face, blk, wide = mean_operator.shape
    fields = field_operators.shape[0]
    shape = (layers, face, (bits + 1) * blk, (face + 2) * blk)
    out = jax.ShapeDtypeStruct(shape, jnp.bfloat16)
    spec = pl.BlockSpec((1, 1) + shape[2:], lambda l, f: (l, f, 0, 0))
    return pl.pallas_call(
        functools.partial(prep_kernel, face, bits, modes_dev),
        grid=(layers, face),
        in_specs=[
            pl.BlockSpec((1, 1, blk, wide), lambda l, f: (l, f, 0, 0)),
            pl.BlockSpec((fields, 1, 1, blk, wide), lambda l, f: (0, l, f, 0, 0)),
            pl.BlockSpec(memory_space=pltpu.SMEM),
            pl.BlockSpec(memory_space=pltpu.SMEM),
        ],
        out_specs=(spec, spec),
        out_shape=(out, out),
        compiler_params=pltpu.CompilerParams(vmem_limit_bytes=VMEM_LIMIT),
    )(mean_operator, field_operators, adjacency, mode_masks)


def solve_kernel(
    peers, spaces, chunks, src, hi_hbm, lo_hbm, x_out, r_out,
    w_hi, w_lo, direction, res, x, split, halo_low, halo_up,
    w_sem, own_sem, in_send, in_recv, low_send, low_recv, up_send, up_recv, out_send, out_recv, own_out,
):
    layers, face = w_hi.shape[:2]
    blk = w_hi.shape[2] // (peers.bit_length())
    bits = peers.bit_length() - 1
    lc = src.shape[3]
    rows = peers * lc
    me = lax.axis_index("mode")
    s = lax.axis_index("space")
    has_low = s > 0
    has_up = s < spaces - 1

    load_hi = pltpu.make_async_copy(hi_hbm, w_hi, w_sem.at[0])
    load_lo = pltpu.make_async_copy(lo_hbm, w_lo, w_sem.at[1])
    load_hi.start()
    load_lo.start()

    barrier = pltpu.get_barrier_semaphore()
    for k in range(1, peers):
        pl.semaphore_signal(barrier, inc=1, device_id={"mode": lax.rem(me + k, peers)}, device_id_type=MESH)

    @pl.when(has_low)
    def _():
        pl.semaphore_signal(barrier, inc=1, device_id={"space": s - 1}, device_id_type=MESH)

    @pl.when(has_up)
    def _():
        pl.semaphore_signal(barrier, inc=1, device_id={"space": s + 1}, device_id_type=MESH)

    pl.semaphore_wait(barrier, peers - 1 + has_low.astype(jnp.int32) + has_up.astype(jnp.int32))

    def slab(ref, c, h):
        return ref.at[c, :, pl.ds(pl.multiple_of(h * lc, lc), lc), :]

    def in_copy(c, k):
        to = lax.rem(me + k, peers)
        return pltpu.make_async_remote_copy(
            src_ref=src.at[to, c], dst_ref=slab(direction.at[0], c, me),
            send_sem=in_send.at[c, k], recv_sem=in_recv.at[c, k],
            device_id={"mode": to}, device_id_type=MESH,
        )

    def in_wait(c, k):
        pltpu.make_async_remote_copy(
            src_ref=src.at[0, c], dst_ref=slab(direction.at[0], c, lax.rem(me + peers - k, peers)),
            send_sem=in_send.at[c, k], recv_sem=in_recv.at[c, k],
            device_id={"mode": lax.rem(me + k, peers)}, device_id_type=MESH,
        ).wait_recv()

    def own_copy(c):
        return pltpu.make_async_copy(src.at[me, c], slab(direction.at[0], c, me), own_sem.at[c])

    def to_low(t, c):
        return pltpu.make_async_remote_copy(
            src_ref=direction.at[lax.rem(t, 2), c, 0], dst_ref=halo_up.at[t, c],
            send_sem=low_send.at[t, c], recv_sem=up_recv.at[t, c],
            device_id={"space": s - 1}, device_id_type=MESH,
        )

    def to_up(t, c):
        return pltpu.make_async_remote_copy(
            src_ref=direction.at[lax.rem(t, 2), c, layers - 1], dst_ref=halo_low.at[t, c],
            send_sem=up_send.at[t, c], recv_sem=low_recv.at[t, c],
            device_id={"space": s + 1}, device_id_type=MESH,
        )

    def halo_start(t, c):
        @pl.when(has_low)
        def _():
            to_low(t, c).start()

        @pl.when(has_up)
        def _():
            to_up(t, c).start()

    def halo_sent(t, c):
        @pl.when(has_low)
        def _():
            to_low(t, c).wait_send()

        @pl.when(has_up)
        def _():
            to_up(t, c).wait_send()

    def halo_arrived(t, c):
        @pl.when(has_low)
        def _():
            to_up(t, c).wait_recv()

        @pl.when(has_up)
        def _():
            to_low(t, c).wait_recv()

    def out_copy(which, ref, out, c, k):
        to = lax.rem(me + k, peers)
        return pltpu.make_async_remote_copy(
            src_ref=slab(ref, c, to), dst_ref=out.at[me, c],
            send_sem=out_send.at[which, c, k], recv_sem=out_recv.at[which, c, k],
            device_id={"mode": to}, device_id_type=MESH,
        )

    def out_own(which, ref, out, c):
        return pltpu.make_async_copy(slab(ref, c, me), out.at[me, c], own_out.at[which, c])

    def out_start(which, ref, out, c):
        for k in range(1, peers):
            out_copy(which, ref, out, c, k).start()
        out_own(which, ref, out, c).start()

    def out_finish(which, ref, out, c):
        for k in range(1, peers):
            came = lax.rem(me + peers - k, peers)
            out_copy(which, ref, out, c, k).wait_send()
            pltpu.make_async_remote_copy(
                src_ref=slab(ref, c, me), dst_ref=out.at[came, c],
                send_sem=out_send.at[which, c, k], recv_sem=out_recv.at[which, c, k],
                device_id={"mode": lax.rem(me + k, peers)}, device_id_type=MESH,
            ).wait_recv()
        out_own(which, ref, out, c).wait()

    for c in range(chunks):
        for k in range(1, peers):
            in_copy(c, k).start()
        own_copy(c).start()

    @pl.when(jnp.logical_not(has_low))
    def _():
        halo_low[...] = jnp.zeros_like(halo_low)

    @pl.when(jnp.logical_not(has_up))
    def _():
        halo_up[...] = jnp.zeros_like(halo_up)

    for c in range(chunks):
        own_copy(c).wait()
        for k in range(1, peers):
            in_wait(c, k)
        halo_start(0, c)
        res[c] = direction[0, c]
        x[c] = direction[0, c]
    load_hi.wait()
    load_lo.wait()

    def keep_split(at, value):
        high = value.astype(jnp.bfloat16)
        split[at, :rows, :] = high
        split[at, rows:, :] = (value - high.astype(jnp.float32)).astype(jnp.bfloat16)

    def product(a, b):
        return lax.dot_general(a, b, (((1,), (1,)), ((), ())), preferred_element_type=jnp.float32)

    sigma = THETA / DELTA

    def step(i, ratio):
        t, c = i // chunks, lax.rem(i, chunks)
        now = lax.rem(t, 2)
        ratio_new = 1.0 / (2.0 * sigma - ratio)
        keep, add = ratio_new * ratio, 2.0 * ratio_new / DELTA
        for l in range(layers):
            keep_split(l + 1, direction[now, c, l])
        halo_arrived(t, c)
        keep_split(0, halo_low[t, c])
        keep_split(layers + 1, halo_up[t, c])

        @pl.when(t > 0)
        def _():
            halo_sent(t - 1, c)

        for l in range(layers):
            for f in range(face):
                lanes = slice(f * blk, (f + 1) * blk)
                a = jnp.concatenate([split[l + 1], split[l, :, lanes], split[l + 2, :, lanes]], axis=1)
                y = product(a, w_hi[l, f])
                y = y[:rows] + y[rows:] + product(a[:rows], w_lo[l, f])
                d = direction[now, c, l, :, lanes]
                total = d + y[:, :blk]
                for b in range(bits):
                    term = y[:, (b + 1) * blk : (b + 2) * blk]
                    total = total + jnp.concatenate(
                        [term[(h ^ (1 << b)) * lc : ((h ^ (1 << b)) + 1) * lc] for h in range(peers)], axis=0
                    )
                r = res[c, l, :, lanes] - total
                res[c, l, :, lanes] = r

                @pl.when(t < DEGREE - 1)
                def _():
                    d_new = keep * d + add * r
                    direction[1 - now, c, l, :, lanes] = d_new
                    x[c, l, :, lanes] = x[c, l, :, lanes] + d_new

        @pl.when(t < DEGREE - 1)
        def _():
            halo_start(t + 1, c)

        @pl.when(t == DEGREE - 2)
        def _():
            out_start(0, x, x_out, c)

        @pl.when(t == DEGREE - 1)
        def _():
            out_start(1, res, r_out, c)

        return jnp.where(c == chunks - 1, ratio_new, ratio)

    lax.fori_loop(0, DEGREE * chunks, step, jnp.float32(1.0 / sigma))

    for c in range(chunks):
        halo_sent(DEGREE - 1, c)
        for k in range(1, peers):
            in_copy(c, k).wait_send()
    for c in range(chunks):
        out_finish(0, x, x_out, c)
        out_finish(1, res, r_out, c)


def per_device(peers, spaces, source_field, mean_operator, field_operators, adjacency, mode_masks):
    layers, face, blk, modes_dev = source_field.shape
    bits = peers.bit_length() - 1
    chunks = CHUNKS
    lc = modes_dev // (peers * chunks)
    rows = peers * lc
    wide = face * blk
    w_hi, w_lo = prepared(mean_operator, field_operators, adjacency, mode_masks, bits, modes_dev)
    src = source_field.reshape(layers, face, blk, peers, chunks, lc)
    src = src.transpose(3, 4, 0, 5, 1, 2).reshape(peers, chunks, layers, lc, wide) / THETA
    out = jax.ShapeDtypeStruct(src.shape, jnp.float32)
    field = pltpu.VMEM((chunks, layers, rows, wide), jnp.float32)
    halo = pltpu.VMEM((DEGREE, chunks, rows, wide), jnp.float32)
    dma = pltpu.SemaphoreType.DMA
    x, r = pl.pallas_call(
        functools.partial(solve_kernel, peers, spaces, chunks),
        in_specs=[
            pl.BlockSpec(memory_space=pltpu.VMEM),
            pl.BlockSpec(memory_space=pl.ANY),
            pl.BlockSpec(memory_space=pl.ANY),
        ],
        out_specs=(pl.BlockSpec(memory_space=pl.ANY), pl.BlockSpec(memory_space=pl.ANY)),
        out_shape=(out, out),
        scratch_shapes=[
            pltpu.VMEM(w_hi.shape, jnp.bfloat16),
            pltpu.VMEM(w_lo.shape, jnp.bfloat16),
            pltpu.VMEM((2, chunks, layers, rows, wide), jnp.float32),
            field,
            field,
            pltpu.VMEM((layers + 2, 2 * rows, wide), jnp.bfloat16),
            halo,
            halo,
            dma((2,)),
            dma((chunks,)),
            dma((chunks, peers)),
            dma((chunks, peers)),
            dma((DEGREE, chunks)),
            dma((DEGREE, chunks)),
            dma((DEGREE, chunks)),
            dma((DEGREE, chunks)),
            dma((2, chunks, peers)),
            dma((2, chunks, peers)),
            dma((2, chunks)),
        ],
        compiler_params=pltpu.CompilerParams(
            collective_id=0, has_side_effects=True, vmem_limit_bytes=VMEM_LIMIT
        ),
    )(src, w_hi, w_lo)

    def back(value):
        value = value.reshape(peers, chunks, layers, lc, face, blk)
        return value.transpose(2, 4, 5, 0, 1, 3).reshape(layers, face, blk, modes_dev)

    return back(x), back(r)


def solution(mesh):
    in_specs = (
        P("space", None, None, "mode"),
        P("space", None, None, None),
        P(None, "space", None, None, None),
        P("space", None, None),
        P(),
    )
    out_specs = (P("space", None, None, "mode"), P("space", None, None, "mode"))
    return jax.shard_map(
        functools.partial(per_device, mesh.shape["mode"], mesh.shape["space"]),
        mesh=mesh, in_specs=in_specs, out_specs=out_specs, check_vma=False,
    )
```

```python
import functools

import jax
import jax.numpy as jnp
from jax import lax
from jax.experimental import pallas as pl
from jax.experimental.pallas import tpu as pltpu
from jax.sharding import PartitionSpec as P

DEGREE = 4
COUPLING = 0.5773502691896258
THETA = 1.0
DELTA = 0.7
CHUNKS = 4
GROUP = 2
VMEM_LIMIT = 66_000_000
MESH = pl.DeviceIdType.MESH


def prepare(raw, e, slot, modes_dev, adj_ref, mask_ref, w_hi, w_lo):
    face, blk = w_hi.shape[1], raw.shape[2]
    layer, f = e // face, lax.rem(e, face)
    for op in range(w_hi.shape[2] // blk):
        if op == 0:
            weights = [None]
        else:
            weights = [
                jnp.where(mask_ref[j] == modes_dev * (1 << (op - 1)), COUPLING, 0.0).astype(jnp.float32)
                for j in range(raw.shape[1] - 1)
            ]

        def block(s):
            lanes = slice(s * blk, (s + 1) * blk)
            if op == 0:
                return raw[slot, 0, :, lanes]
            total = weights[0] * raw[slot, 1, :, lanes]
            for j in range(1, len(weights)):
                total = total + weights[j] * raw[slot, 1 + j, :, lanes]
            return total

        own = block(0)
        sides = [block(3 + s) for s in range(adj_ref.shape[2])]
        parts = []
        for g in range(face):
            total = jnp.where(f == g, 1.0, 0.0).astype(jnp.float32) * own
            for s, side in enumerate(sides):
                total = total + jnp.where(adj_ref[layer, f, s] == g, 1.0, 0.0).astype(jnp.float32) * side
            parts.append(total)
        parts += [block(1), block(2)]
        for at, part in enumerate(parts):
            high = part.astype(jnp.bfloat16)
            low = (part - high.astype(jnp.float32)).astype(jnp.bfloat16)
            w_hi[layer, f, op * blk : (op + 1) * blk, at * blk : (at + 1) * blk] = high
            w_lo[layer, f, op * blk : (op + 1) * blk, at * blk : (at + 1) * blk] = low


def solve_kernel(
    peers, spaces, chunks, modes_dev, src, mean, fields, adj, masks, x_out, r_out,
    raw, w_hi, w_lo, direction, res, x, split, halo_low, halo_up,
    w_sem, own_sem, in_send, in_recv, low_send, low_recv, up_send, up_recv, out_send, out_recv, own_out,
):
    layers, face = w_hi.shape[:2]
    blk = w_hi.shape[2] // (peers.bit_length())
    bits = peers.bit_length() - 1
    lc = src.shape[3]
    rows = peers * lc
    me = lax.axis_index("mode")
    s = lax.axis_index("space")
    has_low = s > 0
    has_up = s < spaces - 1

    elements = layers * face

    def loads(e):
        slot = lax.rem(e, 2)
        l, f = e // face, lax.rem(e, face)
        return (
            pltpu.make_async_copy(mean.at[l, f], raw.at[slot, 0], w_sem.at[slot, 0]),
            pltpu.make_async_copy(fields.at[:, l, f], raw.at[slot, pl.ds(1, fields.shape[0])], w_sem.at[slot, 1]),
        )

    for e in range(2):
        for load in loads(e):
            load.start()

    barrier = pltpu.get_barrier_semaphore()
    for k in range(1, peers):
        pl.semaphore_signal(barrier, inc=1, device_id={"mode": lax.rem(me + k, peers)}, device_id_type=MESH)

    @pl.when(has_low)
    def _():
        pl.semaphore_signal(barrier, inc=1, device_id={"space": s - 1}, device_id_type=MESH)

    @pl.when(has_up)
    def _():
        pl.semaphore_signal(barrier, inc=1, device_id={"space": s + 1}, device_id_type=MESH)

    pl.semaphore_wait(barrier, peers - 1 + has_low.astype(jnp.int32) + has_up.astype(jnp.int32))

    def slab(ref, c, h):
        return ref.at[c, :, pl.ds(pl.multiple_of(h * lc, lc), lc), :]

    def in_copy(c, k):
        to = lax.rem(me + k, peers)
        return pltpu.make_async_remote_copy(
            src_ref=src.at[to, c], dst_ref=slab(direction.at[0], c, me),
            send_sem=in_send.at[c, k], recv_sem=in_recv.at[c, k],
            device_id={"mode": to}, device_id_type=MESH,
        )

    def in_wait(c, k):
        pltpu.make_async_remote_copy(
            src_ref=src.at[0, c], dst_ref=slab(direction.at[0], c, lax.rem(me + peers - k, peers)),
            send_sem=in_send.at[c, k], recv_sem=in_recv.at[c, k],
            device_id={"mode": lax.rem(me + k, peers)}, device_id_type=MESH,
        ).wait_recv()

    def own_copy(c):
        return pltpu.make_async_copy(src.at[me, c], slab(direction.at[0], c, me), own_sem.at[c])

    def to_low(t, c):
        return pltpu.make_async_remote_copy(
            src_ref=direction.at[lax.rem(t, 2), c, 0], dst_ref=halo_up.at[t, c],
            send_sem=low_send.at[t, c], recv_sem=up_recv.at[t, c],
            device_id={"space": s - 1}, device_id_type=MESH,
        )

    def to_up(t, c):
        return pltpu.make_async_remote_copy(
            src_ref=direction.at[lax.rem(t, 2), c, layers - 1], dst_ref=halo_low.at[t, c],
            send_sem=up_send.at[t, c], recv_sem=low_recv.at[t, c],
            device_id={"space": s + 1}, device_id_type=MESH,
        )

    def halo_start(t, c):
        @pl.when(has_low)
        def _():
            to_low(t, c).start()

        @pl.when(has_up)
        def _():
            to_up(t, c).start()

    def halo_sent(t, c):
        @pl.when(has_low)
        def _():
            to_low(t, c).wait_send()

        @pl.when(has_up)
        def _():
            to_up(t, c).wait_send()

    def halo_arrived(t, c):
        @pl.when(has_low)
        def _():
            to_up(t, c).wait_recv()

        @pl.when(has_up)
        def _():
            to_low(t, c).wait_recv()

    def out_copy(which, ref, out, c, k):
        to = lax.rem(me + k, peers)
        return pltpu.make_async_remote_copy(
            src_ref=slab(ref, c, to), dst_ref=out.at[me, c],
            send_sem=out_send.at[which, c, k], recv_sem=out_recv.at[which, c, k],
            device_id={"mode": to}, device_id_type=MESH,
        )

    def out_own(which, ref, out, c):
        return pltpu.make_async_copy(slab(ref, c, me), out.at[me, c], own_out.at[which, c])

    def out_start(which, ref, out, c):
        for k in range(1, peers):
            out_copy(which, ref, out, c, k).start()
        out_own(which, ref, out, c).start()

    def out_finish(which, ref, out, c):
        for k in range(1, peers):
            came = lax.rem(me + peers - k, peers)
            out_copy(which, ref, out, c, k).wait_send()
            pltpu.make_async_remote_copy(
                src_ref=slab(ref, c, me), dst_ref=out.at[came, c],
                send_sem=out_send.at[which, c, k], recv_sem=out_recv.at[which, c, k],
                device_id={"mode": lax.rem(me + k, peers)}, device_id_type=MESH,
            ).wait_recv()
        out_own(which, ref, out, c).wait()

    for c in range(chunks):
        for k in range(1, peers):
            in_copy(c, k).start()
        own_copy(c).start()

    @pl.when(jnp.logical_not(has_low))
    def _():
        halo_low[...] = jnp.zeros_like(halo_low)

    @pl.when(jnp.logical_not(has_up))
    def _():
        halo_up[...] = jnp.zeros_like(halo_up)

    def arrive(c):
        own_copy(c).wait()
        for k in range(1, peers):
            in_wait(c, k)
        halo_start(0, c)
        res[c] = direction[0, c]
        x[c] = direction[0, c]

    def build(e, carry):
        for load in loads(e):
            load.wait()
        prepare(raw, e, lax.rem(e, 2), modes_dev, adj, masks, w_hi, w_lo)

        @pl.when(e + 2 < elements)
        def _():
            for load in loads(e + 2):
                load.start()

        @pl.when(e == elements // 2)
        def _():
            arrive(0)

        return carry

    lax.fori_loop(0, elements, build, 0)
    for c in range(1, min(GROUP, chunks)):
        arrive(c)

    def keep_split(at, value):
        high = value.astype(jnp.bfloat16)
        split[at, :rows, :] = high
        split[at, rows:, :] = (value - high.astype(jnp.float32)).astype(jnp.bfloat16)

    def product(a, b):
        return lax.dot_general(a, b, (((1,), (1,)), ((), ())), preferred_element_type=jnp.float32)

    sigma = THETA / DELTA

    ratios = [1.0 / sigma]
    for _ in range(DEGREE):
        ratios.append(1.0 / (2.0 * sigma - ratios[-1]))
    group = min(GROUP, chunks)
    per_group = DEGREE * group

    def step(i, carry):
        within = lax.rem(i, per_group)
        t = within // group
        c = (i // per_group) * group + lax.rem(within, group)
        now = lax.rem(t, 2)
        keep, add = jnp.float32(0.0), jnp.float32(0.0)
        for at in range(DEGREE):
            keep = jnp.where(t == at, jnp.float32(ratios[at + 1] * ratios[at]), keep)
            add = jnp.where(t == at, jnp.float32(2.0 * ratios[at + 1] / DELTA), add)
        for l in range(layers):
            keep_split(l + 1, direction[now, c, l])
        halo_arrived(t, c)
        keep_split(0, halo_low[t, c])
        keep_split(layers + 1, halo_up[t, c])

        @pl.when(t > 0)
        def _():
            halo_sent(t - 1, c)

        for l in range(layers):
            for f in range(face):
                lanes = slice(f * blk, (f + 1) * blk)
                a = jnp.concatenate([split[l + 1], split[l, :, lanes], split[l + 2, :, lanes]], axis=1)
                y = product(a, w_hi[l, f])
                y = y[:rows] + y[rows:] + product(a[:rows], w_lo[l, f])
                d = direction[now, c, l, :, lanes]
                total = d + y[:, :blk]
                for b in range(bits):
                    term = y[:, (b + 1) * blk : (b + 2) * blk]
                    total = total + jnp.concatenate(
                        [term[(h ^ (1 << b)) * lc : ((h ^ (1 << b)) + 1) * lc] for h in range(peers)], axis=0
                    )
                r = res[c, l, :, lanes] - total
                res[c, l, :, lanes] = r

                @pl.when(t < DEGREE - 1)
                def _():
                    d_new = keep * d + add * r
                    direction[1 - now, c, l, :, lanes] = d_new
                    x[c, l, :, lanes] = x[c, l, :, lanes] + d_new

        @pl.when(t < DEGREE - 1)
        def _():
            halo_start(t + 1, c)

        @pl.when(t == DEGREE - 2)
        def _():
            out_start(0, x, x_out, c)

        @pl.when(t == DEGREE - 1)
        def _():
            out_start(1, res, r_out, c)

        @pl.when(jnp.logical_and(t == DEGREE - 2, c + group < chunks))
        def _():
            arrive(c + group)

        return carry

    lax.fori_loop(0, DEGREE * chunks, step, 0)

    for c in range(chunks):
        halo_sent(DEGREE - 1, c)
        for k in range(1, peers):
            in_copy(c, k).wait_send()
    for c in range(chunks):
        out_finish(0, x, x_out, c)
        out_finish(1, res, r_out, c)


def per_device(peers, spaces, source_field, mean_operator, field_operators, adjacency, mode_masks):
    layers, face, blk, modes_dev = source_field.shape
    bits = peers.bit_length() - 1
    chunks = CHUNKS
    while modes_dev % (peers * chunks * 8):
        chunks //= 2
    lc = modes_dev // (peers * chunks)
    rows = peers * lc
    wide = face * blk
    weights = pltpu.VMEM((layers, face, (bits + 1) * blk, (face + 2) * blk), jnp.bfloat16)
    src = source_field.reshape(layers, face, blk, peers, chunks, lc)
    src = src.transpose(3, 4, 0, 5, 1, 2).reshape(peers, chunks, layers, lc, wide) / THETA
    out = jax.ShapeDtypeStruct(src.shape, jnp.float32)
    field = pltpu.VMEM((chunks, layers, rows, wide), jnp.float32)
    halo = pltpu.VMEM((DEGREE, chunks, rows, wide), jnp.float32)
    dma = pltpu.SemaphoreType.DMA
    x, r = pl.pallas_call(
        functools.partial(solve_kernel, peers, spaces, chunks, modes_dev),
        in_specs=[
            pl.BlockSpec(memory_space=pltpu.VMEM),
            pl.BlockSpec(memory_space=pl.ANY),
            pl.BlockSpec(memory_space=pl.ANY),
            pl.BlockSpec(memory_space=pltpu.SMEM),
            pl.BlockSpec(memory_space=pltpu.SMEM),
        ],
        out_specs=(pl.BlockSpec(memory_space=pl.ANY), pl.BlockSpec(memory_space=pl.ANY)),
        out_shape=(out, out),
        scratch_shapes=[
            pltpu.VMEM((2, 1 + field_operators.shape[0]) + mean_operator.shape[2:], jnp.float32),
            weights,
            weights,
            pltpu.VMEM((2, chunks, layers, rows, wide), jnp.float32),
            field,
            field,
            pltpu.VMEM((layers + 2, 2 * rows, wide), jnp.bfloat16),
            halo,
            halo,
            dma((2, 2)),
            dma((chunks,)),
            dma((chunks, peers)),
            dma((chunks, peers)),
            dma((DEGREE, chunks)),
            dma((DEGREE, chunks)),
            dma((DEGREE, chunks)),
            dma((DEGREE, chunks)),
            dma((2, chunks, peers)),
            dma((2, chunks, peers)),
            dma((2, chunks)),
        ],
        compiler_params=pltpu.CompilerParams(
            collective_id=0, has_side_effects=True, vmem_limit_bytes=VMEM_LIMIT
        ),
    )(src, mean_operator, field_operators, adjacency, mode_masks)

    def back(value):
        value = value.reshape(peers, chunks, layers, lc, face, blk)
        return value.transpose(2, 4, 5, 0, 1, 3).reshape(layers, face, blk, modes_dev)

    return back(x), back(r)


def solution(mesh):
    in_specs = (
        P("space", None, None, "mode"),
        P("space", None, None, None),
        P(None, "space", None, None, None),
        P("space", None, None),
        P(),
    )
    out_specs = (P("space", None, None, "mode"), P("space", None, None, "mode"))
    return jax.shard_map(
        functools.partial(per_device, mesh.shape["mode"], mesh.shape["space"]),
        mesh=mesh, in_specs=in_specs, out_specs=out_specs, check_vma=False,
    )
```

```python
import functools

import jax
import jax.numpy as jnp
from jax import lax
from jax.experimental import pallas as pl
from jax.experimental.pallas import tpu as pltpu
from jax.sharding import PartitionSpec as P

DEGREE = 4
COUPLING = 0.5773502691896258
THETA = 1.0
DELTA = 0.7
CHUNKS = 4
GROUP = 2
LAG = 2
SLOTS = 4
Y_FIRST = True
VMEM_LIMIT = 66_000_000
MESH = pl.DeviceIdType.MESH


def prepare(raw, e, slot, modes_dev, adj_ref, mask_ref, w_hi, w_lo):
    face, blk = w_hi.shape[1], raw.shape[2]
    layer, f = e // face, lax.rem(e, face)
    for op in range(w_hi.shape[3] // blk):
        if op == 0:
            weights = [None]
        else:
            weights = [
                jnp.where(mask_ref[j] == modes_dev * (1 << (op - 1)), COUPLING, 0.0).astype(jnp.float32)
                for j in range(raw.shape[1] - 1)
            ]

        def block(s):
            lanes = slice(s * blk, (s + 1) * blk)
            if op == 0:
                return raw[slot, 0, :, lanes]
            total = weights[0] * raw[slot, 1, :, lanes]
            for j in range(1, len(weights)):
                total = total + weights[j] * raw[slot, 1 + j, :, lanes]
            return total

        own = block(0)
        sides = [block(3 + s) for s in range(adj_ref.shape[2])]
        parts = []
        for g in range(face):
            total = jnp.where(f == g, 1.0, 0.0).astype(jnp.float32) * own
            for s, side in enumerate(sides):
                total = total + jnp.where(adj_ref[layer, f, s] == g, 1.0, 0.0).astype(jnp.float32) * side
            parts.append(total)
        parts += [block(1), block(2)]
        for at, part in enumerate(parts):
            part = part.T
            high = part.astype(jnp.bfloat16)
            low = (part - high.astype(jnp.float32)).astype(jnp.bfloat16)
            w_hi[layer, f, at * blk : (at + 1) * blk, op * blk : (op + 1) * blk] = high
            w_lo[layer, f, at * blk : (at + 1) * blk, op * blk : (op + 1) * blk] = low


def solve_kernel(
    peers, spaces, chunks, modes_dev, src, mean, fields, adj, masks, x_out, r_out,
    raw, w_hi, w_lo, direction, res, x, split, halo_low, halo_up, relay,
    w_sem, own_sem, in_send, in_recv, low_send, low_recv, up_send, up_recv,
    relay_send, relay_recv, forward_send, forward_recv, out_send, out_recv, own_out,
):
    layers, face = w_hi.shape[:2]
    blk = w_hi.shape[3] // (peers.bit_length())
    bits = peers.bit_length() - 1
    lc = src.shape[3]
    rows = peers * lc
    me = lax.axis_index("mode")
    s = lax.axis_index("space")
    has_low = s > 0
    has_up = s < spaces - 1
    relayed = spaces >= 4 and spaces % 2 == 0
    odd = lax.rem(s, 2) == 1
    even = jnp.logical_not(odd)
    half = rows // 2 if relayed else rows

    elements = layers * face

    def loads(e):
        slot = lax.rem(e, SLOTS)
        l, f = e // face, lax.rem(e, face)
        return (
            pltpu.make_async_copy(mean.at[l, f], raw.at[slot, 0], w_sem.at[slot, 0]),
            pltpu.make_async_copy(fields.at[:, l, f], raw.at[slot, pl.ds(1, fields.shape[0])], w_sem.at[slot, 1]),
        )

    for e in range(min(SLOTS, elements)):
        for load in loads(e):
            load.start()

    barrier = pltpu.get_barrier_semaphore()
    for k in range(1, peers):
        pl.semaphore_signal(barrier, inc=1, device_id={"mode": lax.rem(me + k, peers)}, device_id_type=MESH)

    @pl.when(has_low)
    def _():
        pl.semaphore_signal(barrier, inc=1, device_id={"space": s - 1}, device_id_type=MESH)

    @pl.when(has_up)
    def _():
        pl.semaphore_signal(barrier, inc=1, device_id={"space": s + 1}, device_id_type=MESH)

    expected = peers - 1 + has_low.astype(jnp.int32) + has_up.astype(jnp.int32)
    if relayed:
        far_low, far_up = s >= 2, s < spaces - 2
        expected = expected + far_low.astype(jnp.int32) + far_up.astype(jnp.int32)

        @pl.when(far_low)
        def _():
            pl.semaphore_signal(barrier, inc=1, device_id={"space": s - 2}, device_id_type=MESH)

        @pl.when(far_up)
        def _():
            pl.semaphore_signal(barrier, inc=1, device_id={"space": s + 2}, device_id_type=MESH)

    pl.semaphore_wait(barrier, expected)

    def slab(ref, c, h):
        return ref.at[c, :, pl.ds(pl.multiple_of(h * lc, lc), lc), :]

    def in_copy(c, k):
        to = lax.rem(me + k, peers)
        return pltpu.make_async_remote_copy(
            src_ref=src.at[to, c], dst_ref=slab(direction.at[0], c, me),
            send_sem=in_send.at[c, k], recv_sem=in_recv.at[c, k],
            device_id={"mode": to}, device_id_type=MESH,
        )

    def in_wait(c, k):
        pltpu.make_async_remote_copy(
            src_ref=src.at[0, c], dst_ref=slab(direction.at[0], c, lax.rem(me + peers - k, peers)),
            send_sem=in_send.at[c, k], recv_sem=in_recv.at[c, k],
            device_id={"mode": lax.rem(me + k, peers)}, device_id_type=MESH,
        ).wait_recv()

    def own_copy(c):
        return pltpu.make_async_copy(src.at[me, c], slab(direction.at[0], c, me), own_sem.at[c])

    def to_low(t, c, count):
        return pltpu.make_async_remote_copy(
            src_ref=direction.at[lax.rem(t, 2), c, 0, pl.ds(0, count)], dst_ref=halo_up.at[t, c, pl.ds(0, count)],
            send_sem=low_send.at[t, c], recv_sem=up_recv.at[t, c],
            device_id={"space": s - 1}, device_id_type=MESH,
        )

    def to_up(t, c, count):
        return pltpu.make_async_remote_copy(
            src_ref=direction.at[lax.rem(t, 2), c, layers - 1, pl.ds(0, count)],
            dst_ref=halo_low.at[t, c, pl.ds(0, count)],
            send_sem=up_send.at[t, c], recv_sem=low_recv.at[t, c],
            device_id={"space": s + 1}, device_id_type=MESH,
        )

    def to_relay(t, c, layer, offset):
        return pltpu.make_async_remote_copy(
            src_ref=direction.at[lax.rem(t, 2), c, layer, pl.ds(half, rows - half)], dst_ref=relay.at[t, c],
            send_sem=relay_send.at[t, c], recv_sem=relay_recv.at[t, c],
            device_id={"space": s + offset}, device_id_type=MESH,
        )

    def forward(t, c, halo, offset):
        return pltpu.make_async_remote_copy(
            src_ref=relay.at[t, c], dst_ref=halo.at[t, c, pl.ds(half, rows - half)],
            send_sem=forward_send.at[t, c], recv_sem=forward_recv.at[t, c],
            device_id={"space": s + offset}, device_id_type=MESH,
        )

    both = jnp.logical_and
    up_offset, low_offset = (2, -2) if Y_FIRST else (-1, 1)
    if relayed:
        whole_low, whole_up = both(odd, has_low), both(even, has_up)
        part_low, part_up = both(even, has_low), both(odd, has_up)
    else:
        whole_low, whole_up = has_low, has_up

    def halo_each(t, c, act):
        @pl.when(whole_low)
        def _():
            act(to_low(t, c, rows))

        @pl.when(whole_up)
        def _():
            act(to_up(t, c, rows))

        if relayed:

            @pl.when(part_low)
            def _():
                act(to_relay(t, c, 0, low_offset))
                act(to_low(t, c, half))

            @pl.when(part_up)
            def _():
                act(to_relay(t, c, layers - 1, up_offset))
                act(to_up(t, c, half))

    def halo_start(t, c):
        halo_each(t, c, lambda copy: copy.start())

    def halo_sent(t, c):
        halo_each(t, c, lambda copy: copy.wait_send())

    def forward_each(t, c, act):
        if relayed:

            @pl.when(both(odd, s >= 3))
            def _():
                act(forward(t, c, *((halo_low, -1) if Y_FIRST else (halo_up, -2))))

            @pl.when(both(even, s < spaces - 3))
            def _():
                act(forward(t, c, *((halo_up, 1) if Y_FIRST else (halo_low, 2))))

    def halo_forward(t, c):
        if relayed:

            @pl.when(jnp.logical_or(both(odd, s >= 3), both(even, s < spaces - 3)))
            def _():
                to_relay(t, c, 0, jnp.where(odd, -1, 1)).wait_recv()

            forward_each(t, c, lambda copy: copy.start())

    def halo_arrived(t, c):
        if not relayed:

            @pl.when(has_low)
            def _():
                to_up(t, c, rows).wait_recv()

            @pl.when(has_up)
            def _():
                to_low(t, c, rows).wait_recv()

            return

        @pl.when(both(odd, has_low))
        def _():
            to_up(t, c, rows).wait_recv()

        @pl.when(both(even, has_up))
        def _():
            to_low(t, c, rows).wait_recv()

        @pl.when(both(even, has_low))
        def _():
            to_up(t, c, half).wait_recv()
            forward(t, c, halo_low, -1).wait_recv()

        @pl.when(both(odd, has_up))
        def _():
            to_low(t, c, half).wait_recv()
            forward(t, c, halo_up, 1).wait_recv()

    def out_copy(which, ref, out, c, k):
        to = lax.rem(me + k, peers)
        return pltpu.make_async_remote_copy(
            src_ref=slab(ref, c, to), dst_ref=out.at[me, c],
            send_sem=out_send.at[which, c, k], recv_sem=out_recv.at[which, c, k],
            device_id={"mode": to}, device_id_type=MESH,
        )

    def out_own(which, ref, out, c):
        return pltpu.make_async_copy(slab(ref, c, me), out.at[me, c], own_out.at[which, c])

    def out_start(which, ref, out, c):
        for k in range(1, peers):
            out_copy(which, ref, out, c, k).start()
        out_own(which, ref, out, c).start()

    def out_finish(which, ref, out, c):
        for k in range(1, peers):
            came = lax.rem(me + peers - k, peers)
            out_copy(which, ref, out, c, k).wait_send()
            pltpu.make_async_remote_copy(
                src_ref=slab(ref, c, me), dst_ref=out.at[came, c],
                send_sem=out_send.at[which, c, k], recv_sem=out_recv.at[which, c, k],
                device_id={"mode": lax.rem(me + k, peers)}, device_id_type=MESH,
            ).wait_recv()
        out_own(which, ref, out, c).wait()

    for c in range(chunks):
        for k in range(1, peers):
            in_copy(c, k).start()
        own_copy(c).start()

    @pl.when(jnp.logical_not(has_low))
    def _():
        halo_low[...] = jnp.zeros_like(halo_low)

    @pl.when(jnp.logical_not(has_up))
    def _():
        halo_up[...] = jnp.zeros_like(halo_up)

    def arrive(c):
        own_copy(c).wait()
        for k in range(1, peers):
            in_wait(c, k)
        halo_start(0, c)
        res[c] = direction[0, c]
        x[c] = direction[0, c]

    def build(e, carry):
        for load in loads(e):
            load.wait()
        prepare(raw, e, lax.rem(e, SLOTS), modes_dev, adj, masks, w_hi, w_lo)

        @pl.when(e + SLOTS < elements)
        def _():
            for load in loads(e + SLOTS):
                load.start()

        @pl.when(e == elements // 2)
        def _():
            arrive(0)

        return carry

    lax.fori_loop(0, elements, build, 0)
    group = min(GROUP, chunks)
    for c in range(1, group):
        arrive(c)

    def keep_split(at, value):
        high = value.astype(jnp.bfloat16)
        split[at, :rows, :] = high
        split[at, rows:, :] = (value - high.astype(jnp.float32)).astype(jnp.bfloat16)

    def product(a, b):
        return lax.dot_general(a, b, (((1,), (0,)), ((), ())), preferred_element_type=jnp.float32)

    sigma = THETA / DELTA

    ratios = [1.0 / sigma]
    for _ in range(DEGREE):
        ratios.append(1.0 / (2.0 * sigma - ratios[-1]))
    order = []
    arrivals = {}
    for turn in range(DEGREE + LAG * (chunks // group - 1)):
        for place in range(group):
            for c in range(place, chunks, group):
                t = turn - LAG * (c // group)
                if 0 <= t < DEGREE:
                    order.append((t, c))
        for c in range(group, chunks):
            if turn == max(LAG * (c // group) - 1, 0):
                arrivals[c] = len(order) - 1


    def step(i, carry):
        t, c = jnp.int32(0), jnp.int32(0)
        for at, (t_at, c_at) in enumerate(order):
            t = jnp.where(i == at, t_at, t)
            c = jnp.where(i == at, c_at, c)
        now = lax.rem(t, 2)
        keep, add = jnp.float32(0.0), jnp.float32(0.0)
        for at in range(DEGREE):
            keep = jnp.where(t == at, jnp.float32(ratios[at + 1] * ratios[at]), keep)
            add = jnp.where(t == at, jnp.float32(2.0 * ratios[at + 1] / DELTA), add)
        for l in range(layers):
            keep_split(l + 1, direction[now, c, l])
        halo_forward(t, c)
        halo_arrived(t, c)
        keep_split(0, halo_low[t, c])
        keep_split(layers + 1, halo_up[t, c])

        @pl.when(t > 0)
        def _():
            halo_sent(t - 1, c)

        for l in range(layers):
            for f in range(face):
                lanes = slice(f * blk, (f + 1) * blk)
                a = jnp.concatenate([split[l + 1], split[l, :, lanes], split[l + 2, :, lanes]], axis=1)
                y = product(a, w_hi[l, f])
                y = y[:rows] + y[rows:] + product(a[:rows], w_lo[l, f])
                d = direction[now, c, l, :, lanes]
                total = d + y[:, :blk]
                for b in range(bits):
                    term = y[:, (b + 1) * blk : (b + 2) * blk]
                    total = total + jnp.concatenate(
                        [term[(h ^ (1 << b)) * lc : ((h ^ (1 << b)) + 1) * lc] for h in range(peers)], axis=0
                    )
                r = res[c, l, :, lanes] - total
                res[c, l, :, lanes] = r

                @pl.when(t < DEGREE - 1)
                def _():
                    d_new = keep * d + add * r
                    direction[1 - now, c, l, :, lanes] = d_new
                    x[c, l, :, lanes] = x[c, l, :, lanes] + d_new

        @pl.when(t < DEGREE - 1)
        def _():
            halo_start(t + 1, c)

        @pl.when(t == DEGREE - 2)
        def _():
            out_start(0, x, x_out, c)

        @pl.when(t == DEGREE - 1)
        def _():
            out_start(1, res, r_out, c)

        for late, at in arrivals.items():

            @pl.when(i == at)
            def _():
                arrive(late)

        return carry

    lax.fori_loop(0, DEGREE * chunks, step, 0)

    for c in range(chunks):
        halo_sent(DEGREE - 1, c)
        for t in range(DEGREE):
            forward_each(t, c, lambda copy: copy.wait_send())
        for k in range(1, peers):
            in_copy(c, k).wait_send()
    for c in range(chunks):
        out_finish(0, x, x_out, c)
        out_finish(1, res, r_out, c)


def per_device(peers, spaces, source_field, mean_operator, field_operators, adjacency, mode_masks):
    layers, face, blk, modes_dev = source_field.shape
    bits = peers.bit_length() - 1
    chunks = CHUNKS
    while modes_dev % (peers * chunks * 8):
        chunks //= 2
    lc = modes_dev // (peers * chunks)
    rows = peers * lc
    wide = face * blk
    weights = pltpu.VMEM((layers, face, (face + 2) * blk, (bits + 1) * blk), jnp.bfloat16)
    src = source_field.reshape(layers, face, blk, peers, chunks, lc)
    src = src.transpose(3, 4, 0, 5, 1, 2).reshape(peers, chunks, layers, lc, wide) / THETA
    out = jax.ShapeDtypeStruct(src.shape, jnp.float32)
    field = pltpu.VMEM((chunks, layers, rows, wide), jnp.float32)
    halo = pltpu.VMEM((DEGREE, chunks, rows, wide), jnp.float32)
    dma = pltpu.SemaphoreType.DMA
    x, r = pl.pallas_call(
        functools.partial(solve_kernel, peers, spaces, chunks, modes_dev),
        in_specs=[
            pl.BlockSpec(memory_space=pltpu.VMEM),
            pl.BlockSpec(memory_space=pl.ANY),
            pl.BlockSpec(memory_space=pl.ANY),
            pl.BlockSpec(memory_space=pltpu.SMEM),
            pl.BlockSpec(memory_space=pltpu.SMEM),
        ],
        out_specs=(pl.BlockSpec(memory_space=pl.ANY), pl.BlockSpec(memory_space=pl.ANY)),
        out_shape=(out, out),
        scratch_shapes=[
            pltpu.VMEM((SLOTS, 1 + field_operators.shape[0]) + mean_operator.shape[2:], jnp.float32),
            weights,
            weights,
            pltpu.VMEM((2, chunks, layers, rows, wide), jnp.float32),
            field,
            field,
            pltpu.VMEM((layers + 2, 2 * rows, wide), jnp.bfloat16),
            halo,
            halo,
            pltpu.VMEM((DEGREE, chunks, rows // 2, wide), jnp.float32),
            dma((SLOTS, 2)),
            dma((chunks,)),
            dma((chunks, peers)),
            dma((chunks, peers)),
            dma((DEGREE, chunks)),
            dma((DEGREE, chunks)),
            dma((DEGREE, chunks)),
            dma((DEGREE, chunks)),
            dma((DEGREE, chunks)),
            dma((DEGREE, chunks)),
            dma((DEGREE, chunks)),
            dma((DEGREE, chunks)),
            dma((2, chunks, peers)),
            dma((2, chunks, peers)),
            dma((2, chunks)),
        ],
        compiler_params=pltpu.CompilerParams(
            collective_id=0, has_side_effects=True, vmem_limit_bytes=VMEM_LIMIT
        ),
    )(src, mean_operator, field_operators, adjacency, mode_masks)

    def back(value):
        value = value.reshape(peers, chunks, layers, lc, face, blk)
        return value.transpose(2, 4, 5, 0, 1, 3).reshape(layers, face, blk, modes_dev)

    return back(x), back(r)


def solution(mesh):
    in_specs = (
        P("space", None, None, "mode"),
        P("space", None, None, None),
        P(None, "space", None, None, None),
        P("space", None, None),
        P(),
    )
    out_specs = (P("space", None, None, "mode"), P("space", None, None, "mode"))
    return jax.shard_map(
        functools.partial(per_device, mesh.shape["mode"], mesh.shape["space"]),
        mesh=mesh, in_specs=in_specs, out_specs=out_specs, check_vma=False,
    )
```
